32 devices in a mesh: groups: 2 (over x), tensor: 16 (over z, y, core).
Axes of the slice: x: 2, y: 2, z: 4, core: 2. Of those that a mesh axis runs over, the one named last changes fastest.
Arguments:
- tokens: bfloat16 [64, 8192], P(('groups', 'tensor')), parts along dimension 0, may hold values from -6 to 6
- gate_weight: bfloat16 [8192, 28672], P(None, 'tensor'), may hold values from -0.0625 to 0.0625
- up_weight: bfloat16 [8192, 28672], P(None, 'tensor'), may hold values from -0.0625 to 0.0625
- down_weight: bfloat16 [28672, 8192], P('tensor'), may hold values from -0.03125 to 0.03125
Outputs:
- mixed: bfloat16 [64, 8192], P(('groups', 'tensor')), parts along dimension 0
The draws below stay inside these ranges and needn't reach their ends.
There are 2 independent parts, one for each index of `groups`. The reference program is written for one: setup_inputs(seed, part) draws one part's arguments, and reference() takes and returns one part's arrays. A program takes and returns all parts, laid end to end along the dimension named above; an argument that names none is the same for every part. Nothing has to cross between parts.
All inputs are finite; a program needn't handle non-finite values.
Results may differ from the reference program's by a relative error of at most 0.015.
Values may be sent and summed in bfloat16 or wider, within the bound.
A program may use at most 128 MiB of HBM per device.

```python
import jax
import jax.numpy as jnp
import numpy as np
from jax import lax

D = 8192
FF = 28672
BLOCK = 32
TOKENS = 32
N_TENSOR = 16


def level_of(own_key, shape, pieces, low, top_value):
    def one(position, shards_of):
        heights = jax.random.uniform(jax.random.fold_in(jax.random.fold_in(own_key, 6), position), (shards_of,), jnp.float32, low / len(pieces), top_value / len(pieces))
        return jnp.repeat(jnp.exp(heights), shape[position] // shards_of).reshape((-1,) + (1,) * (len(shape) - position - 1))

    factor_of = one(*pieces[0])
    for cut in pieces[1:]:
        factor_of = factor_of * one(*cut)
    return factor_of


def normal_values(key, dims, spread, reach, pieces=(), kind=jnp.bfloat16):
    result = spread * jax.random.normal(key, dims, jnp.float32)
    if pieces:
        result = result * level_of(key, dims, pieces, -0.22, 0.18)
    return jnp.clip(result, -reach, reach).astype(kind)


def setup_inputs(seed: int = 0, part: int = 0) -> dict:
    keys = jax.random.split(jax.random.key(seed), 5)
    part_keys = jax.random.split(jax.random.fold_in(keys[4], part), 5)
    return {
        "tokens": normal_values(part_keys[0], (TOKENS, D), 1.0, 6.0, ((0, 16),)),
        "gate_weight": normal_values(keys[1], (D, FF), D ** -0.5, 0.0625, ((1, 16),)),
        "up_weight": normal_values(keys[2], (D, FF), D ** -0.5, 0.0625, ((1, 16),)),
        "down_weight": normal_values(keys[3], (FF, D), FF ** -0.5, 0.03125, ((0, 16),)),
    }


def walsh(order):
    index = np.arange(order)
    common = index[:, None] & index[None, :]
    parity = common * 0
    for shift in range(max(order.bit_length(), 1)):
        parity = parity ^ common >> shift & 1
    return (1 - 2 * parity).astype(np.float32)

def reference(tokens, gate_weight, up_weight, down_weight):
    gate = jnp.dot(tokens, gate_weight, preferred_element_type=jnp.float32)
    up = jnp.dot(tokens, up_weight, preferred_element_type=jnp.float32)
    hidden = jax.nn.silu(gate) * up
    width = FF // N_TENSOR
    shaped = hidden.reshape(TOKENS, N_TENSOR, width // BLOCK, BLOCK)
    outer = jnp.asarray(walsh(N_TENSOR), jnp.float32)
    inner = jnp.asarray(walsh(BLOCK), jnp.float32)
    turned = jnp.einsum('pq,tqbr,rs->tpbs', outer, shaped, inner, precision=lax.Precision.HIGHEST)
    turned = turned * (1.0 / np.sqrt(N_TENSOR * BLOCK))
    rotated = turned.reshape(TOKENS, FF).astype(jnp.bfloat16)
    return jnp.dot(rotated, down_weight, preferred_element_type=jnp.float32).astype(jnp.bfloat16)
```

```python
import functools

import jax
import jax.numpy as jnp
import numpy as np
from jax import lax
from jax.experimental import pallas as pl
from jax.experimental.pallas import tpu as pltpu
from jax.sharding import PartitionSpec as P

BLOCK = 32
COLS = 128
SPLIT = 4
CHUNKS = 4
GROUP = 2
PLANE = 4
MESH = pl.DeviceIdType.MESH


def swapped(value, axis, stride):
    mask = 2**stride
    pairs = [(source, source ^ mask) for source in range(lax.axis_size(axis))]
    return lax.ppermute(value, axis, pairs)


def walsh(order):
    index = np.arange(order)
    common = index[:, None] & index[None, :]
    parity = common * 0
    for shift in range(max(order.bit_length(), 1)):
        parity = parity ^ common >> shift & 1
    return (1 - 2 * parity).astype(np.float32)


def plain(tokens, gate_weight, up_weight, down_weight):
    devices = lax.axis_size("tensor")
    width = gate_weight.shape[1]
    scale = 1.0 / np.sqrt(devices * BLOCK)
    inner = jnp.asarray(walsh(BLOCK), jnp.float32)
    piece = lax.all_gather(tokens, "tensor", axis=0, tiled=True)
    gate = jnp.dot(piece, gate_weight, preferred_element_type=jnp.float32)
    up = jnp.dot(piece, up_weight, preferred_element_type=jnp.float32)
    hidden = jax.nn.silu(gate) * up
    total = hidden.shape[0]
    local = jnp.einsum(
        "tbr,rs->tbs",
        hidden.reshape(total, width // BLOCK, BLOCK),
        inner,
        precision=lax.Precision.HIGHEST,
    ).reshape(total, width)
    index = lax.axis_index("tensor")
    for level in range(devices.bit_length() - 1):
        partner = swapped(local.astype(jnp.bfloat16), "tensor", level).astype(local.dtype)
        upper = index // (1 << level) % 2
        local = jnp.where(upper == 1, partner - local, local + partner)
    rotated = (local * scale).astype(jnp.bfloat16)
    terms = jnp.dot(rotated, down_weight, preferred_element_type=jnp.float32)
    mixed = lax.psum_scatter(terms, "tensor", scatter_dimension=0, tiled=True)
    return mixed.astype(jnp.bfloat16)


def parity(value, bits):
    total = value & 1
    for shift in range(1, bits):
        total = total ^ ((value >> shift) & 1)
    return total


def kernel(
    n,
    tokens,
    gate,
    up,
    down,
    out,
    gathered,
    lhs,
    acc,
    weights,
    downs,
    signs,
    hidden,
    first_out,
    first_in,
    middle,
    second_out,
    second_in,
    rotated,
    half_out,
    half_in,
    piece_out,
    piece_in,
    weight_sem,
    down_sem,
    gather_send,
    gather_recv,
    first_send,
    first_recv,
    second_send,
    second_recv,
    half_send,
    half_recv,
    piece_send,
    piece_recv,
):
    f32, bf16 = jnp.float32, jnp.bfloat16
    me = lax.axis_index("tensor")
    mine = lax.axis_index("groups")
    own, depth = tokens.shape
    total = n * own
    part = gate.shape[1] // 2
    blocks = part // COLS
    outs = down.shape[1]
    bits = n.bit_length() - 1
    ring = n // PLANE
    scale = float(1.0 / np.sqrt(n * BLOCK))
    deep = depth // SPLIT

    def device(j, mask):
        return {"groups": mine ^ j, "tensor": me ^ mask}

    def slot(j, mask):
        q = me ^ mask
        return (mine ^ j) * n + (q & 1) * (n // 2) + (q >> 1)

    def remote(source, target, send_sem, recv_sem, j, mask):
        return pltpu.make_async_remote_copy(
            src_ref=source,
            dst_ref=target,
            send_sem=send_sem,
            recv_sem=recv_sem,
            device_id=device(j, mask),
            device_id_type=MESH,
        )

    plane = [(j, m) for j in range(2) for m in range(PLANE) if j or m]
    line = [(0, PLANE * k) for k in range(1, ring)]

    barrier = pltpu.get_barrier_semaphore()
    for j, mask in plane + line:
        pl.semaphore_signal(barrier, inc=1, device_id=device(j, mask), device_id_type=MESH)

    def weight_copy(which, b):
        source = (gate, up)[which]
        start = pl.multiple_of(mine * part + b * COLS, COLS)
        return pltpu.make_async_copy(
            source.at[:, pl.ds(start, COLS)],
            weights.at[b, :, pl.ds(which * COLS, COLS)],
            weight_sem.at[b, which],
        )

    def down_copy(b, j):
        start = pl.multiple_of((mine ^ j) * part + b * COLS, COLS)
        return pltpu.make_async_copy(
            down.at[pl.ds(start, COLS)], downs.at[pl.ds((2 * b + j) * COLS, COLS)], down_sem.at[b, j]
        )

    for b in range(blocks):
        for which in range(2):
            weight_copy(which, b).start()

    pl.semaphore_wait(barrier, len(plane) + len(line))

    sends = []

    def send(source, place, origin, j, mask):
        oj, om = origin[0] ^ j, origin[1] ^ mask
        copy = remote(
            source,
            gathered.at[place],
            gather_send.at[len(sends)],
            gather_recv.at[oj * n + om],
            j,
            mask,
        )
        copy.start()
        sends.append(copy)

    def arrived(j, mask):
        place = slot(j, mask)
        remote(
            gathered.at[place], gathered.at[place], gather_send.at[0], gather_recv.at[j * n + mask], 0, 1
        ).wait_recv()
        return place

    here = slot(0, 0)
    near = [(1, 0), (0, 2), (1, 2)]
    for j, mask in line[::-1] + near + [(0, 1)]:
        send(tokens, here, (0, 0), j, mask)
    gathered[here] = tokens[...]

    one = lax.broadcasted_iota(jnp.int32, (COLS, COLS), 0)
    two = lax.broadcasted_iota(jnp.int32, (COLS, COLS), 1)
    sign = (1 - 2 * parity(one & two & (BLOCK - 1), BLOCK.bit_length() - 1)).astype(f32)
    signs[...] = jnp.where((one // BLOCK) == (two // BLOCK), sign, 0.0).astype(bf16)

    def to_core(j, mask):
        place = arrived(j, mask)
        send(gathered.at[place], place, (j, mask), 0, 1)

    def spread(k):
        place = arrived(0, PLANE * k)
        for j, mask in near + [(0, 1)]:
            send(gathered.at[place], place, (0, PLANE * k), j, mask)

    for k in range(1, ring):
        spread(k)
        if k == 1:
            for j, mask in near:
                to_core(j, mask)
    for b in range(blocks):
        for j in range(2):
            down_copy(b, j).start()
    for k in range(1, ring):
        for j, mask in near:
            to_core(j, PLANE * k + mask)
    for k in range(ring):
        for j, mask in [(0, 1), (1, 1), (0, 3), (1, 3)]:
            arrived(j, PLANE * k + mask)

    @pl.loop(0, depth // 1024)
    def _(c):
        columns = pl.ds(pl.multiple_of(c * 1024, 1024), 1024)
        lhs[:, columns] = gathered[:, :, columns].reshape(2 * total, 1024)

    groups = [(lo, min(lo + GROUP, blocks)) for lo in range(0, blocks, GROUP)]

    def first_copy(g, j, m):
        lo, hi = groups[g]
        columns = pl.ds(lo * COLS, (hi - lo) * COLS)
        place = j * PLANE + m
        return remote(
            first_out.at[mine ^ j, :, columns],
            first_in.at[place, :, columns],
            first_send.at[g, place],
            first_recv.at[g, place],
            j,
            m,
        )

    def second_copy(g, k):
        lo, hi = groups[g]
        columns = pl.ds(2 * lo * COLS, 2 * (hi - lo) * COLS)
        return remote(
            second_out.at[:, columns],
            second_in.at[k, :, columns],
            second_send.at[g, k],
            second_recv.at[g, k],
            0,
            PLANE * k,
        )

    def flip(mask, kept):
        return (1 - 2 * parity(me & (me ^ mask) & kept, bits)).astype(f32)

    plane_flips = [flip(m, PLANE - 1) for m in range(PLANE)]
    line_flips = [flip(PLANE * k, n - PLANE) * scale for k in range(ring)]

    def block(b):
        left = jnp.zeros((2 * total, COLS), f32)
        right = jnp.zeros((2 * total, COLS), f32)
        for which in range(2):
            weight_copy(which, b).wait()
        for piece in range(SPLIT):
            rows_of = pl.ds(piece * deep, deep)
            left += jnp.dot(lhs[:, rows_of], weights[b, rows_of, :COLS], preferred_element_type=f32)
            right += jnp.dot(lhs[:, rows_of], weights[b, rows_of, COLS:], preferred_element_type=f32)
        value = left / (1.0 + jnp.exp(-left)) * right
        high = value.astype(bf16)
        low = (value - high.astype(f32)).astype(bf16)
        value = jnp.dot(high, signs[...], preferred_element_type=f32) + jnp.dot(
            low, signs[...], preferred_element_type=f32
        )
        columns = pl.ds(b * COLS, COLS)
        for j in range(2):
            hidden[j, :, columns] = value[j * total : (j + 1) * total]
            first_out[j, :, columns] = value[j * total : (j + 1) * total].astype(bf16)

    for g, (lo, hi) in enumerate(groups):
        for b in range(lo, hi):
            block(b)
        for j, m in plane[::-1]:
            first_copy(g, j, m).start()

    for g, (lo, hi) in enumerate(groups):
        for j, m in plane:
            first_copy(g, j, m).wait_recv()
        for b in range(lo, hi):
            columns = pl.ds(b * COLS, COLS)
            for j in range(2):
                value = None
                for m in range(PLANE):
                    if j or m:
                        piece = first_in[j * PLANE + m, :, columns].astype(f32)
                    else:
                        piece = hidden[mine, :, columns]
                    piece = piece * plane_flips[m]
                    value = piece if value is None else value + piece
                target = pl.ds((2 * b + j) * COLS, COLS)
                middle[:, target] = value
                second_out[:, target] = value.astype(bf16)
        for k in range(ring - 1, 0, -1):
            second_copy(g, k).start()

    def rotate(g):
        lo, hi = groups[g]
        for k in range(1, ring):
            second_copy(g, k).wait_recv()
        for b in range(2 * lo, 2 * hi):
            columns = pl.ds(b * COLS, COLS)
            value = middle[:, columns] * line_flips[0]
            for k in range(1, ring):
                value = value + second_in[k, :, columns].astype(f32) * line_flips[k]
            rotated[:, columns] = value.astype(bf16)
        for b in range(lo, hi):
            for j in range(2):
                down_copy(b, j).wait()

    def product(g, columns):
        lo, hi = groups[g]
        rows_of = pl.ds(2 * lo * COLS, 2 * (hi - lo) * COLS)
        return jnp.dot(rotated[:, rows_of], downs[rows_of, columns], preferred_element_type=f32)

    last = len(groups) - 1
    for g in range(last):
        rotate(g)

        @pl.loop(0, outs // 2048)
        def _(c):
            columns = pl.ds(pl.multiple_of(c * 2048, 2048), 2048)
            term = product(g, columns)
            if g:
                term = acc[:, columns] + term
            acc[:, columns] = term

    size = outs // CHUNKS
    half = total // 2
    pieces = n // 2
    place = me >> 1
    kept = pl.ds(pl.multiple_of((me & 1) * half, half), half)
    given = pl.ds(pl.multiple_of((1 - (me & 1)) * half, half), half)

    def half_copy(c):
        columns = pl.ds(c * size, size)
        return remote(
            half_out.at[:, columns], half_in.at[:, columns], half_send.at[c], half_recv.at[c], 0, 1
        )

    def piece_copy(c, k):
        columns = pl.ds(c * size, size)
        return remote(
            piece_out.at[place ^ k, :, columns],
            piece_in.at[k, :, columns],
            piece_send.at[c, k],
            piece_recv.at[c, k],
            0,
            2 * k,
        )

    rotate(last)
    for c in range(CHUNKS):
        columns = pl.ds(c * size, size)
        acc[:, columns] = acc[:, columns] + product(last, columns)
        half_out[:, columns] = acc[given, columns].astype(bf16)
        half_copy(c).start()
    for c in range(CHUNKS):
        columns = pl.ds(c * size, size)
        half_copy(c).wait_recv()
        term = acc[kept, columns] + half_in[:, columns].astype(f32)
        piece_out[:, :, columns] = term.astype(bf16).reshape(pieces, own, size)
        for k in range(pieces - 1, 0, -1):
            piece_copy(c, k).start()
    for c in range(CHUNKS):
        columns = pl.ds(c * size, size)
        term = piece_out[place, :, columns].astype(f32)
        for k in range(1, pieces):
            piece_copy(c, k).wait_recv()
            term = term + piece_in[k, :, columns].astype(f32)
        out[:, columns] = term.astype(bf16)

    for copy in sends:
        copy.wait_send()
    for g in range(len(groups)):
        for j, m in plane:
            first_copy(g, j, m).wait_send()
        for k in range(1, ring):
            second_copy(g, k).wait_send()
    for c in range(CHUNKS):
        half_copy(c).wait_send()
        for k in range(1, pieces):
            piece_copy(c, k).wait_send()


def fused(n, tokens, gate_weight, up_weight, down_weight):
    own, depth = tokens.shape
    total = n * own
    part = gate_weight.shape[1] // 2
    blocks = part // COLS
    outs = down_weight.shape[1]
    ring = n // PLANE
    pieces = n // 2
    groups = pl.cdiv(blocks, GROUP)
    bf16, f32 = jnp.bfloat16, jnp.float32
    vmem = pl.BlockSpec(memory_space=pltpu.VMEM)
    anywhere = pl.BlockSpec(memory_space=pl.ANY)
    dma = pltpu.SemaphoreType.DMA
    sent = (ring - 1) * 5 + 4 + (PLANE - 1) * ring
    return pl.pallas_call(
        functools.partial(kernel, n),
        out_shape=jax.ShapeDtypeStruct((own, outs), bf16),
        in_specs=[vmem, anywhere, anywhere, anywhere],
        out_specs=vmem,
        scratch_shapes=[
            pltpu.VMEM((2 * n, own, depth), bf16),
            pltpu.VMEM((2 * total, depth), bf16),
            pltpu.VMEM((total, outs), f32),
            pltpu.VMEM((blocks, depth, 2 * COLS), bf16),
            pltpu.VMEM((2 * part, outs), bf16),
            pltpu.VMEM((COLS, COLS), bf16),
            pltpu.VMEM((2, total, part), f32),
            pltpu.VMEM((2, total, part), bf16),
            pltpu.VMEM((2 * PLANE, total, part), bf16),
            pltpu.VMEM((total, 2 * part), f32),
            pltpu.VMEM((total, 2 * part), bf16),
            pltpu.VMEM((ring, total, 2 * part), bf16),
            pltpu.VMEM((total, 2 * part), bf16),
            pltpu.VMEM((total // 2, outs), bf16),
            pltpu.VMEM((total // 2, outs), bf16),
            pltpu.VMEM((pieces, own, outs), bf16),
            pltpu.VMEM((pieces, own, outs), bf16),
            dma((blocks, 2)),
            dma((blocks, 2)),
            dma((sent,)),
            dma((2 * n,)),
            dma((groups, 2 * PLANE)),
            dma((groups, 2 * PLANE)),
            dma((groups, ring)),
            dma((groups, ring)),
            dma((CHUNKS,)),
            dma((CHUNKS,)),
            dma((CHUNKS, pieces)),
            dma((CHUNKS, pieces)),
        ],
        compiler_params=pltpu.CompilerParams(
            collective_id=0, has_side_effects=True, vmem_limit_bytes=67_000_000
        ),
    )(tokens, gate_weight, up_weight, down_weight)


def per_device(tokens, gate_weight, up_weight, down_weight):
    n, parts = lax.axis_size("tensor"), lax.axis_size("groups")
    own, depth = tokens.shape
    width, outs = gate_weight.shape[1], down_weight.shape[1]
    total = n * own
    held = 2 * (width * (depth + outs) + 4 * total * (depth + outs) + 20 * total * width)
    fits = (
        parts == 2
        and 8 <= n
        and n & (n - 1) == 0
        and width % (2 * COLS) == 0
        and width // (2 * COLS) > GROUP
        and total % 32 == 0
        and total <= 64
        and depth % (1024 * SPLIT) == 0
        and outs % (2048 * CHUNKS) == 0
        and held <= 68_000_000
    )
    if fits:
        return fused(n, tokens, gate_weight, up_weight, down_weight)
    return plain(tokens, gate_weight, up_weight, down_weight)


def solution(mesh):
    return jax.shard_map(
        per_device,
        mesh=mesh,
        in_specs=(
            P(("groups", "tensor"), None),
            P(None, "tensor"),
            P(None, "tensor"),
            P("tensor", None),
        ),
        out_specs=P(("groups", "tensor"), None),
        check_vma=False,
    )
```

```python
import functools

import jax
import jax.numpy as jnp
import numpy as np
from jax import lax
from jax.experimental import pallas as pl
from jax.experimental.pallas import tpu as pltpu
from jax.sharding import PartitionSpec as P

BLOCK = 32
COLS = 128
SPLIT = 4
CHUNKS = 4
GROUP = 2
LAG = 1
QUADS = (0, 3)
PLANE = 4
MESH = pl.DeviceIdType.MESH


def swapped(value, axis, stride):
    mask = 2**stride
    pairs = [(source, source ^ mask) for source in range(lax.axis_size(axis))]
    return lax.ppermute(value, axis, pairs)


def walsh(order):
    index = np.arange(order)
    common = index[:, None] & index[None, :]
    parity = common * 0
    for shift in range(max(order.bit_length(), 1)):
        parity = parity ^ common >> shift & 1
    return (1 - 2 * parity).astype(np.float32)


def plain(tokens, gate_weight, up_weight, down_weight):
    devices = lax.axis_size("tensor")
    width = gate_weight.shape[1]
    scale = 1.0 / np.sqrt(devices * BLOCK)
    inner = jnp.asarray(walsh(BLOCK), jnp.float32)
    piece = lax.all_gather(tokens, "tensor", axis=0, tiled=True)
    gate = jnp.dot(piece, gate_weight, preferred_element_type=jnp.float32)
    up = jnp.dot(piece, up_weight, preferred_element_type=jnp.float32)
    hidden = jax.nn.silu(gate) * up
    total = hidden.shape[0]
    local = jnp.einsum(
        "tbr,rs->tbs",
        hidden.reshape(total, width // BLOCK, BLOCK),
        inner,
        precision=lax.Precision.HIGHEST,
    ).reshape(total, width)
    index = lax.axis_index("tensor")
    for level in range(devices.bit_length() - 1):
        partner = swapped(local.astype(jnp.bfloat16), "tensor", level).astype(local.dtype)
        upper = index // (1 << level) % 2
        local = jnp.where(upper == 1, partner - local, local + partner)
    rotated = (local * scale).astype(jnp.bfloat16)
    terms = jnp.dot(rotated, down_weight, preferred_element_type=jnp.float32)
    mixed = lax.psum_scatter(terms, "tensor", scatter_dimension=0, tiled=True)
    return mixed.astype(jnp.bfloat16)


def parity(value, bits):
    total = value & 1
    for shift in range(1, bits):
        total = total ^ ((value >> shift) & 1)
    return total


def kernel(
    n,
    tokens,
    gate,
    up,
    down,
    out,
    gathered,
    lhs,
    acc,
    weights,
    downs,
    signs,
    hidden,
    core_out,
    core_in,
    first_out,
    first_in,
    middle,
    second_out,
    second_in,
    rotated,
    half_out,
    half_in,
    piece_out,
    piece_in,
    weight_sem,
    down_sem,
    gather_sem,
    core_sem,
    first_sem,
    second_sem,
    half_sem,
    piece_sem,
    send_sem,
    known,
):
    f32, bf16 = jnp.float32, jnp.bfloat16
    me = lax.axis_index("tensor")
    mine = lax.axis_index("groups")
    own, depth = tokens.shape
    total = n * own
    part = gate.shape[1] // 2
    blocks = part // COLS
    outs = down.shape[1]
    bits = n.bit_length() - 1
    ring = n // PLANE
    levels = ring.bit_length() - 1
    scale = float(1.0 / np.sqrt(n * BLOCK))
    deep = depth // SPLIT
    groups = [(lo, min(lo + GROUP, blocks)) for lo in range(0, blocks, GROUP)]
    every = range(len(groups))
    at_gather, at_core, at_first, at_half, at_piece, at_second = range(6)
    quads = [g in QUADS or levels == 1 for g in every]

    def device(j, mask):
        return {"groups": mine ^ j, "tensor": me ^ mask}

    def slot(j, mask):
        q = me ^ mask
        return (mine ^ j) * n + (q & 1) * (n // 2) + (q >> 1)

    def remote(source, target, sent, received, j, mask):
        return pltpu.make_async_remote_copy(
            src_ref=source,
            dst_ref=target,
            send_sem=send_sem.at[sent],
            recv_sem=received,
            device_id=device(j, mask),
            device_id_type=MESH,
        )

    plane = [(j, m) for j in range(2) for m in range(PLANE) if j or m]
    line = [(0, PLANE * k) for k in range(1, ring)]

    barrier = pltpu.get_barrier_semaphore()
    greeted = plane + line[:2]
    for j, mask in greeted:
        pl.semaphore_signal(barrier, inc=1, device_id=device(j, mask), device_id_type=MESH)

    for g, (lo, hi) in enumerate(groups):
        for b in range(lo, hi):
            start = pl.multiple_of(mine * part + b * COLS, COLS)
            for which, source in enumerate((gate, up)):
                pltpu.make_async_copy(
                    source.at[:, pl.ds(start, COLS)],
                    weights.at[b, :, pl.ds(which * COLS, COLS)],
                    weight_sem.at[g],
                ).start()

    def down_rows(g):
        lo, hi = groups[g]
        return pl.ds(2 * lo * COLS, 2 * (hi - lo) * COLS)

    def start_downs():
        for g, (lo, hi) in enumerate(groups):
            for b in range(lo, hi):
                for j in range(2):
                    start = pl.multiple_of((mine ^ j) * part + b * COLS, COLS)
                    pltpu.make_async_copy(
                        down.at[pl.ds(start, COLS)],
                        downs.at[pl.ds((2 * b + j) * COLS, COLS)],
                        down_sem.at[g],
                    ).start()

    pl.semaphore_wait(barrier, len(greeted))
    for j, mask in line[2:]:
        pl.semaphore_signal(known, inc=1, device_id=device(0, PLANE), device_id_type=MESH)

    near = [(1, 0), (0, 2), (1, 2)]
    across = near[:2]
    diagonal = near[2]
    ours = ring
    aside = 2 * ring
    last_sem = 2 * ring + 1
    kinds = {}
    for k in range(ring):
        for j, m in [(0, 0)] + near:
            if (j, m) == (0, 0):
                kind = k
            elif (j, m) != diagonal:
                kind = ours + k
            else:
                kind = aside if k else 0
            kinds[j, PLANE * k + m] = kind
            kinds[j, PLANE * k + m ^ 1] = last_sem
    sends = []

    def send(origin, j, mask):
        place = slot(*origin)
        kind = kinds[origin[0] ^ j, origin[1] ^ mask]
        source = gathered.at[place] if any(origin) else tokens
        remote(source, gathered.at[place], at_gather, gather_sem.at[kind], j, mask).start()
        sends.append(origin)

    def arrived(kind, count):
        some = gathered.at[pl.ds(0, count)]
        remote(some, some, at_gather, gather_sem.at[kind], 0, 1).wait_recv()

    for j, mask in [diagonal] + line[:2][::-1] + across + [(0, 1)]:
        send((0, 0), j, mask)
    gathered[slot(0, 0)] = tokens[...]
    for j, mask in line[2:]:
        pl.semaphore_wait(known, 1)
        send((0, 0), j, mask)

    one = lax.broadcasted_iota(jnp.int32, (COLS, COLS), 0)
    two = lax.broadcasted_iota(jnp.int32, (COLS, COLS), 1)
    sign = (1 - 2 * parity(one & two & (BLOCK - 1), BLOCK.bit_length() - 1)).astype(f32)
    signs[...] = jnp.where((one // BLOCK) == (two // BLOCK), sign, 0.0).astype(bf16)

    def spread(k):
        arrived(k, 1)
        for j, mask in across:
            send((0, PLANE * k), j, mask)
        if k == ring - 1:
            for j, mask in across:
                send((0, PLANE * k), j, mask ^ 1)
        send((0, PLANE * k), 0, 1)

    def from_across(k):
        arrived(ours + k, 2)
        if k == 0 or k < ring - 1:
            for j, mask in across:
                send((j, PLANE * k + mask), 0, 1)

    spread(1)
    arrived(0, 1)
    for j, mask in line[::-1] + [(0, 1)]:
        send(diagonal, j, mask)
    from_across(0)
    for k in range(2, ring):
        spread(k)
    start_downs()
    for k in range(1, ring):
        from_across(k)
    arrived(aside, ring - 1)
    for k in range(1, ring):
        send((diagonal[0], PLANE * k + diagonal[1]), 0, 1)
    arrived(last_sem, n)

    for g, (lo, hi) in enumerate(groups):
        some = weights.at[lo:hi]
        pltpu.make_async_copy(some, some, weight_sem.at[g]).wait()

    @pl.loop(0, depth // 1024)
    def _(c):
        columns = pl.ds(pl.multiple_of(c * 1024, 1024), 1024)
        lhs[:, columns] = gathered[:, :, columns].reshape(2 * total, 1024)

    def core_copy(b):
        columns = pl.ds(b * COLS, COLS)
        return remote(
            core_out.at[:, :, columns], core_in.at[:, :, columns], at_core, core_sem.at[b], 0, 1
        )

    def first_columns(g):
        lo, hi = groups[g]
        return pl.ds(lo * COLS, (hi - lo) * COLS)

    def second_copy(g, level):
        columns = down_rows(g)
        return remote(
            second_out.at[level, :, columns],
            second_in.at[level, :, columns],
            at_second + g,
            second_sem.at[g, level],
            0,
            PLANE << level,
        )

    def quad_copy(g, k):
        columns = down_rows(g)
        return remote(
            second_out.at[0, :, columns],
            second_in.at[k - 1, :, columns],
            at_second + g,
            second_sem.at[g, 0],
            0,
            PLANE * k,
        )

    def flip(mask):
        return (1 - 2 * parity(me & mask, bits)).astype(f32)

    core_flip, row_flip = flip(1), flip(2)
    line_flips = [flip(PLANE << level) for level in range(levels)]

    def project(b):
        left = jnp.zeros((2 * total, COLS), f32)
        right = jnp.zeros((2 * total, COLS), f32)
        for piece in range(SPLIT):
            rows_of = pl.ds(piece * deep, deep)
            left += jnp.dot(lhs[:, rows_of], weights[b, rows_of, :COLS], preferred_element_type=f32)
            right += jnp.dot(lhs[:, rows_of], weights[b, rows_of, COLS:], preferred_element_type=f32)
        return left, right

    def block(b, left, right):
        value = left / (1.0 + jnp.exp(-left)) * right
        high = value.astype(bf16)
        low = (value - high.astype(f32)).astype(bf16)
        value = jnp.dot(high, signs[...], preferred_element_type=f32) + jnp.dot(
            low, signs[...], preferred_element_type=f32
        )
        columns = pl.ds(b * COLS, COLS)
        for j in range(2):
            hidden[j, :, columns] = value[j * total : (j + 1) * total]
            core_out[j, :, columns] = value[j * total : (j + 1) * total].astype(bf16)
        core_copy(b).start()

    def join(b):
        core_copy(b).wait_recv()
        columns = pl.ds(b * COLS, COLS)
        for j in range(2):
            value = hidden[j, :, columns] * core_flip + core_in[j, :, columns].astype(f32)
            hidden[j, :, columns] = value
            first_out[j, :, columns] = value.astype(bf16)
        for g, (lo, hi) in enumerate(groups):
            if b == hi - 1:
                for place in (2, 0, 1):
                    j, m = near[place]
                    remote(
                        first_out.at[mine ^ j, :, first_columns(g)],
                        first_in.at[place, :, first_columns(g)],
                        at_first,
                        first_sem.at[g],
                        j,
                        m,
                    ).start()

    def meet(g):
        some = first_in.at[:, :, first_columns(g)]
        remote(some, some, at_first, first_sem.at[g], 0, 1).wait_recv()
        for b in range(*groups[g]):
            columns = pl.ds(b * COLS, COLS)
            pair = [
                hidden[mine, :, columns] * row_flip + first_in[1, :, columns].astype(f32),
                first_in[0, :, columns].astype(f32) * row_flip + first_in[2, :, columns].astype(f32),
            ]
            for j, value in enumerate(pair):
                target = pl.ds((2 * b + j) * COLS, COLS)
                middle[:, target] = value
                second_out[0, :, target] = value.astype(bf16)
        if quads[g]:
            for k in range(ring - 1, 0, -1):
                quad_copy(g, k).start()
        else:
            second_copy(g, 0).start()

    def gain(mask):
        return (1 - 2 * parity(me & (me ^ mask) & (n - PLANE), bits)).astype(f32) * scale

    gains = [gain(PLANE * k) for k in range(ring)]

    def turn_quad(g):
        some = second_in.at[:, :, down_rows(g)]
        remote(some, some, at_second + g, second_sem.at[g, 0], 0, PLANE).wait_recv()
        for b in range(2 * groups[g][0], 2 * groups[g][1]):
            columns = pl.ds(b * COLS, COLS)
            value = middle[:, columns] * gains[0]
            for k in range(1, ring):
                value = value + second_in[k - 1, :, columns].astype(f32) * gains[k]
            rotated[:, columns] = value.astype(bf16)

    def turn(g, level):
        lo, hi = groups[g]
        second_copy(g, level).wait_recv()
        for b in range(2 * lo, 2 * hi):
            columns = pl.ds(b * COLS, COLS)
            value = middle[:, columns] * line_flips[level]
            value = value + second_in[level, :, columns].astype(f32)
            if level == levels - 1:
                rotated[:, columns] = (value * scale).astype(bf16)
            else:
                middle[:, columns] = value
                second_out[level + 1, :, columns] = value.astype(bf16)
        if level < levels - 1:
            second_copy(g, level + 1).start()

    ready = project(0)
    for b in range(blocks):
        later = project(b + 1) if b + 1 < blocks else None
        block(b, *ready)
        ready = later
        if b >= LAG:
            join(b - LAG)
    for b in range(max(blocks - LAG, 0), blocks):
        join(b)

    steps = [(0.6 * hi + 3.0 * stage, stage, g) for stage in range(levels) for g, (_, hi) in enumerate(groups)]
    for _, stage, g in sorted(steps):
        if stage:
            if not quads[g]:
                turn(g, stage - 1)
        else:
            meet(g)

    def rotate(g):
        if quads[g]:
            turn_quad(g)
        else:
            turn(g, levels - 1)
        some = downs.at[down_rows(g)]
        pltpu.make_async_copy(some, some, down_sem.at[g]).wait()

    def product(g, columns):
        return jnp.dot(rotated[:, down_rows(g)], downs[down_rows(g), columns], preferred_element_type=f32)

    final = len(groups) - 1
    for g in range(final):
        rotate(g)
        for c in range(outs // 1024):
            columns = pl.ds(c * 1024, 1024)
            term = product(g, columns)
            if g:
                term = acc[:, columns] + term
            acc[:, columns] = term

    size = outs // CHUNKS
    half = total // 2
    pieces = n // 2
    place = me >> 1
    kept = pl.ds(pl.multiple_of((me & 1) * half, half), half)
    given = pl.ds(pl.multiple_of((1 - (me & 1)) * half, half), half)

    def half_copy(c):
        columns = pl.ds(c * size, size)
        return remote(half_out.at[:, columns], half_in.at[:, columns], at_half, half_sem.at[c], 0, 1)

    rotate(final)
    for c in range(CHUNKS):
        columns = pl.ds(c * size, size)
        acc[:, columns] = acc[:, columns] + product(final, columns)
        half_out[:, columns] = acc[given, columns].astype(bf16)
        half_copy(c).start()
    for c in range(CHUNKS):
        columns = pl.ds(c * size, size)
        half_copy(c).wait_recv()
        term = acc[kept, columns] + half_in[:, columns].astype(f32)
        piece_out[:, :, columns] = term.astype(bf16).reshape(pieces, own, size)
        for k in range(pieces - 1, 0, -1):
            remote(
                piece_out.at[place ^ k, :, columns],
                piece_in.at[k, :, columns],
                at_piece,
                piece_sem.at[c],
                0,
                2 * k,
            ).start()
    others = pl.ds(1, pieces - 1)
    for c in range(CHUNKS):
        columns = pl.ds(c * size, size)
        some = piece_in.at[others, :, columns]
        remote(some, some, at_piece, piece_sem.at[c], 0, 2).wait_recv()
        term = piece_out[place, :, columns].astype(f32)
        for k in range(1, pieces):
            term = term + piece_in[k, :, columns].astype(f32)
        out[:, columns] = term.astype(bf16)

    for which, some in [
        (at_gather, gathered.at[pl.ds(0, len(sends))]),
        (at_core, core_out),
        (at_first, first_in),
        (at_half, half_out),
        (at_piece, piece_in.at[others]),
    ]:
        remote(some, some, which, core_sem.at[0], 0, 1).wait_send()
    for g in every:
        some = (second_in if quads[g] else second_out).at[:, :, down_rows(g)]
        remote(some, some, at_second + g, core_sem.at[0], 0, 1).wait_send()


def fused(n, tokens, gate_weight, up_weight, down_weight):
    own, depth = tokens.shape
    total = n * own
    part = gate_weight.shape[1] // 2
    blocks = part // COLS
    outs = down_weight.shape[1]
    ring = n // PLANE
    levels = ring.bit_length() - 1
    pieces = n // 2
    groups = pl.cdiv(blocks, GROUP)
    bf16, f32 = jnp.bfloat16, jnp.float32
    vmem = pl.BlockSpec(memory_space=pltpu.VMEM)
    anywhere = pl.BlockSpec(memory_space=pl.ANY)
    dma = pltpu.SemaphoreType.DMA
    return pl.pallas_call(
        functools.partial(kernel, n),
        out_shape=jax.ShapeDtypeStruct((own, outs), bf16),
        in_specs=[vmem, anywhere, anywhere, anywhere],
        out_specs=vmem,
        scratch_shapes=[
            pltpu.VMEM((2 * n, own, depth), bf16),
            pltpu.VMEM((2 * total, depth), bf16),
            pltpu.VMEM((total, outs), f32),
            pltpu.VMEM((blocks, depth, 2 * COLS), bf16),
            pltpu.VMEM((2 * part, outs), bf16),
            pltpu.VMEM((COLS, COLS), bf16),
            pltpu.VMEM((2, total, part), f32),
            pltpu.VMEM((2, total, part), bf16),
            pltpu.VMEM((2, total, part), bf16),
            pltpu.VMEM((2, total, part), bf16),
            pltpu.VMEM((3, total, part), bf16),
            pltpu.VMEM((total, 2 * part), f32),
            pltpu.VMEM((levels, total, 2 * part), bf16),
            pltpu.VMEM((ring - 1, total, 2 * part), bf16),
            pltpu.VMEM((total, 2 * part), bf16),
            pltpu.VMEM((total // 2, outs), bf16),
            pltpu.VMEM((total // 2, outs), bf16),
            pltpu.VMEM((pieces, own, outs), bf16),
            pltpu.VMEM((pieces, own, outs), bf16),
            dma((groups,)),
            dma((groups,)),
            dma((2 * ring + 2,)),
            dma((blocks,)),
            dma((groups,)),
            dma((groups, levels)),
            dma((CHUNKS,)),
            dma((CHUNKS,)),
            dma((5 + groups,)),
            pltpu.SemaphoreType.REGULAR,
        ],
        compiler_params=pltpu.CompilerParams(
            collective_id=0, has_side_effects=True, vmem_limit_bytes=67_000_000
        ),
    )(tokens, gate_weight, up_weight, down_weight)


def per_device(tokens, gate_weight, up_weight, down_weight):
    n, parts = lax.axis_size("tensor"), lax.axis_size("groups")
    own, depth = tokens.shape
    width, outs = gate_weight.shape[1], down_weight.shape[1]
    total = n * own
    held = 2 * (width * (depth + outs) + 4 * total * (depth + outs) + 20 * total * width)
    fits = (
        parts == 2
        and n in (8, 16)
        and width % (2 * COLS) == 0
        and width // (2 * COLS) > GROUP
        and total % 32 == 0
        and total <= 64
        and depth % (1024 * SPLIT) == 0
        and outs % (2048 * CHUNKS) == 0
        and held <= 68_000_000
    )
    if fits:
        return fused(n, tokens, gate_weight, up_weight, down_weight)
    return plain(tokens, gate_weight, up_weight, down_weight)


def solution(mesh):
    return jax.shard_map(
        per_device,
        mesh=mesh,
        in_specs=(
            P(("groups", "tensor"), None),
            P(None, "tensor"),
            P(None, "tensor"),
            P("tensor", None),
        ),
        out_specs=P(("groups", "tensor"), None),
        check_vma=False,
    )
```

```python
import functools

import jax
import jax.numpy as jnp
import numpy as np
from jax import lax
from jax.experimental import pallas as pl
from jax.experimental.pallas import tpu as pltpu
from jax.sharding import PartitionSpec as P

BLOCK = 32
COLS = 128
SPLIT = 4
CHUNKS = 4
GROUP = 2
LAG = 1
QUADS = (0, 2, 3)
WIDE = 128
PLANE = 4
MESH = pl.DeviceIdType.MESH


def swapped(value, axis, stride):
    mask = 2**stride
    pairs = [(source, source ^ mask) for source in range(lax.axis_size(axis))]
    return lax.ppermute(value, axis, pairs)


def walsh(order):
    index = np.arange(order)
    common = index[:, None] & index[None, :]
    parity = common * 0
    for shift in range(max(order.bit_length(), 1)):
        parity = parity ^ common >> shift & 1
    return (1 - 2 * parity).astype(np.float32)


def plain(tokens, gate_weight, up_weight, down_weight):
    devices = lax.axis_size("tensor")
    width = gate_weight.shape[1]
    scale = 1.0 / np.sqrt(devices * BLOCK)
    inner = jnp.asarray(walsh(BLOCK), jnp.float32)
    piece = lax.all_gather(tokens, "tensor", axis=0, tiled=True)
    gate = jnp.dot(piece, gate_weight, preferred_element_type=jnp.float32)
    up = jnp.dot(piece, up_weight, preferred_element_type=jnp.float32)
    hidden = jax.nn.silu(gate) * up
    total = hidden.shape[0]
    local = jnp.einsum(
        "tbr,rs->tbs",
        hidden.reshape(total, width // BLOCK, BLOCK),
        inner,
        precision=lax.Precision.HIGHEST,
    ).reshape(total, width)
    index = lax.axis_index("tensor")
    for level in range(devices.bit_length() - 1):
        partner = swapped(local.astype(jnp.bfloat16), "tensor", level).astype(local.dtype)
        upper = index // (1 << level) % 2
        local = jnp.where(upper == 1, partner - local, local + partner)
    rotated = (local * scale).astype(jnp.bfloat16)
    terms = jnp.dot(rotated, down_weight, preferred_element_type=jnp.float32)
    mixed = lax.psum_scatter(terms, "tensor", scatter_dimension=0, tiled=True)
    return mixed.astype(jnp.bfloat16)


def parity(value, bits):
    total = value & 1
    for shift in range(1, bits):
        total = total ^ ((value >> shift) & 1)
    return total


def kernel(
    n,
    tokens,
    gate,
    up,
    down,
    out,
    gathered,
    lhs,
    acc,
    weights,
    downs,
    signs,
    hidden,
    core_out,
    core_in,
    first_out,
    first_in,
    middle,
    second_out,
    second_in,
    rotated,
    result,
    half_out,
    half_in,
    piece_out,
    piece_in,
    weight_sem,
    down_sem,
    gather_sem,
    core_sem,
    first_sem,
    second_sem,
    half_sem,
    piece_sem,
    send_sem,
    own_sem,
    known,
):
    f32, bf16 = jnp.float32, jnp.bfloat16
    me = lax.axis_index("tensor")
    mine = lax.axis_index("groups")
    own, depth = tokens.shape
    total = n * own
    part = gate.shape[1] // 2
    blocks = part // COLS
    outs = down.shape[1]
    bits = n.bit_length() - 1
    ring = n // PLANE
    levels = ring.bit_length() - 1
    scale = float(1.0 / np.sqrt(n * BLOCK))
    deep = depth // SPLIT
    groups = [(lo, min(lo + GROUP, blocks)) for lo in range(0, blocks, GROUP)]
    every = range(len(groups))
    at_gather, at_core, at_first, at_half, at_piece, at_second = range(6)
    quads = [g in QUADS or levels == 1 for g in every]

    def device(j, mask):
        return {"groups": mine ^ j, "tensor": me ^ mask}

    def slot(j, mask):
        q = me ^ mask
        return (mine ^ j) * n + (q & 1) * (n // 2) + (q >> 1)

    def remote(source, target, sent, received, j, mask):
        return pltpu.make_async_remote_copy(
            src_ref=source,
            dst_ref=target,
            send_sem=send_sem.at[sent],
            recv_sem=received,
            device_id=device(j, mask),
            device_id_type=MESH,
        )

    plane = [(j, m) for j in range(2) for m in range(PLANE) if j or m]
    line = [(0, PLANE * k) for k in range(1, ring)]

    barrier = pltpu.get_barrier_semaphore()
    greeted = plane + line[:2]
    for j, mask in greeted:
        pl.semaphore_signal(barrier, inc=1, device_id=device(j, mask), device_id_type=MESH)
    loaded = pltpu.make_async_copy(tokens, gathered.at[slot(0, 0)], own_sem.at[0])
    loaded.start()
    loaded.wait()

    for g, (lo, hi) in enumerate(groups):
        for b in range(lo, hi):
            start = pl.multiple_of(mine * part + b * COLS, COLS)
            for which, source in enumerate((gate, up)):
                pltpu.make_async_copy(
                    source.at[:, pl.ds(start, COLS)],
                    weights.at[b, :, pl.ds(which * COLS, COLS)],
                    weight_sem.at[g],
                ).start()

    def down_rows(g):
        lo, hi = groups[g]
        return pl.ds(2 * lo * COLS, 2 * (hi - lo) * COLS)

    def start_downs():
        for g, (lo, hi) in enumerate(groups):
            for b in range(lo, hi):
                for j in range(2):
                    start = pl.multiple_of((mine ^ j) * part + b * COLS, COLS)
                    pltpu.make_async_copy(
                        down.at[pl.ds(start, COLS)],
                        downs.at[pl.ds((2 * b + j) * COLS, COLS)],
                        down_sem.at[g],
                    ).start()

    pl.semaphore_wait(barrier, len(greeted))
    for j, mask in line[2:]:
        pl.semaphore_signal(known, inc=1, device_id=device(0, PLANE), device_id_type=MESH)

    near = [(1, 0), (0, 2), (1, 2)]
    across = near[:2]
    diagonal = near[2]
    ours = ring
    aside = 2 * ring
    last_sem = 2 * ring + 1
    kinds = {}
    for k in range(ring):
        for j, m in [(0, 0)] + near:
            if (j, m) == (0, 0):
                kind = k
            elif (j, m) != diagonal:
                kind = ours + k
            else:
                kind = aside if k else 0
            kinds[j, PLANE * k + m] = kind
            kinds[j, PLANE * k + m ^ 1] = last_sem
    sends = []

    def send(origin, j, mask):
        place = slot(*origin)
        kind = kinds[origin[0] ^ j, origin[1] ^ mask]
        remote(gathered.at[place], gathered.at[place], at_gather, gather_sem.at[kind], j, mask).start()
        sends.append(origin)

    def arrived(kind, count):
        some = gathered.at[pl.ds(0, count)]
        remote(some, some, at_gather, gather_sem.at[kind], 0, 1).wait_recv()

    for j, mask in [diagonal] + line[:2][::-1] + across + [(0, 1)]:
        send((0, 0), j, mask)
    for j, mask in line[2:]:
        pl.semaphore_wait(known, 1)
        send((0, 0), j, mask)

    one = lax.broadcasted_iota(jnp.int32, (COLS, COLS), 0)
    two = lax.broadcasted_iota(jnp.int32, (COLS, COLS), 1)
    sign = (1 - 2 * parity(one & two & (BLOCK - 1), BLOCK.bit_length() - 1)).astype(f32)
    signs[...] = jnp.where((one // BLOCK) == (two // BLOCK), sign, 0.0).astype(bf16)

    def spread(k):
        arrived(k, 1)
        for j, mask in across:
            send((0, PLANE * k), j, mask)
        if k == ring - 1:
            for j, mask in across:
                send((0, PLANE * k), j, mask ^ 1)
        send((0, PLANE * k), 0, 1)

    def from_across(k):
        arrived(ours + k, 2)
        if k == 0 or k < ring - 1:
            for j, mask in across:
                send((j, PLANE * k + mask), 0, 1)

    spread(1)
    arrived(0, 1)
    for j, mask in line[::-1] + [(0, 1)]:
        send(diagonal, j, mask)
    from_across(0)
    for k in range(2, ring):
        spread(k)
    start_downs()
    for k in range(1, ring):
        from_across(k)
    arrived(aside, ring - 1)
    for k in range(1, ring):
        send((diagonal[0], PLANE * k + diagonal[1]), 0, 1)
    arrived(last_sem, n)

    for g, (lo, hi) in enumerate(groups):
        some = weights.at[lo:hi]
        pltpu.make_async_copy(some, some, weight_sem.at[g]).wait()

    @pl.loop(0, depth // 1024)
    def _(c):
        columns = pl.ds(pl.multiple_of(c * 1024, 1024), 1024)
        lhs[:, columns] = gathered[:, :, columns].reshape(2 * total, 1024)

    def core_copy(b):
        columns = pl.ds(b * COLS, COLS)
        return remote(
            core_out.at[:, :, columns], core_in.at[:, :, columns], at_core, core_sem.at[b], 0, 1
        )

    def first_columns(g):
        lo, hi = groups[g]
        return pl.ds(lo * COLS, (hi - lo) * COLS)

    def second_copy(g, level):
        columns = down_rows(g)
        return remote(
            second_out.at[level, :, columns],
            second_in.at[level, :, columns],
            at_second + g,
            second_sem.at[g, level],
            0,
            PLANE << level,
        )

    def quad_copy(g, k):
        columns = down_rows(g)
        return remote(
            second_out.at[0, :, columns],
            second_in.at[k - 1, :, columns],
            at_second + g,
            second_sem.at[g, 0],
            0,
            PLANE * k,
        )

    def flip(mask):
        return (1 - 2 * parity(me & mask, bits)).astype(f32)

    core_flip, row_flip = flip(1), flip(2)
    line_flips = [flip(PLANE << level) for level in range(levels)]

    def project(b):
        left = jnp.zeros((2 * total, COLS), f32)
        right = jnp.zeros((2 * total, COLS), f32)
        for piece in range(SPLIT):
            rows_of = pl.ds(piece * deep, deep)
            left += jnp.dot(lhs[:, rows_of], weights[b, rows_of, :COLS], preferred_element_type=f32)
            right += jnp.dot(lhs[:, rows_of], weights[b, rows_of, COLS:], preferred_element_type=f32)
        return left, right

    def block(b, left, right):
        value = left / (1.0 + jnp.exp(-left)) * right
        high = value.astype(bf16)
        low = (value - high.astype(f32)).astype(bf16)
        value = jnp.dot(high, signs[...], preferred_element_type=f32) + jnp.dot(
            low, signs[...], preferred_element_type=f32
        )
        columns = pl.ds(b * COLS, COLS)
        for j in range(2):
            hidden[j, :, columns] = value[j * total : (j + 1) * total]
            core_out[j, :, columns] = value[j * total : (j + 1) * total].astype(bf16)
        core_copy(b).start()

    def join(b):
        core_copy(b).wait_recv()
        columns = pl.ds(b * COLS, COLS)
        for j in range(2):
            value = hidden[j, :, columns] * core_flip + core_in[j, :, columns].astype(f32)
            hidden[j, :, columns] = value
            first_out[j, :, columns] = value.astype(bf16)
        for g, (lo, hi) in enumerate(groups):
            if b == hi - 1:
                for place in (2, 0, 1):
                    j, m = near[place]
                    remote(
                        first_out.at[mine ^ j, :, first_columns(g)],
                        first_in.at[place, :, first_columns(g)],
                        at_first,
                        first_sem.at[g],
                        j,
                        m,
                    ).start()

    def meet(g):
        some = first_in.at[:, :, first_columns(g)]
        remote(some, some, at_first, first_sem.at[g], 0, 1).wait_recv()
        for b in range(*groups[g]):
            columns = pl.ds(b * COLS, COLS)
            pair = [
                hidden[mine, :, columns] * row_flip + first_in[1, :, columns].astype(f32),
                first_in[0, :, columns].astype(f32) * row_flip + first_in[2, :, columns].astype(f32),
            ]
            for j, value in enumerate(pair):
                target = pl.ds((2 * b + j) * COLS, COLS)
                middle[:, target] = value
                second_out[0, :, target] = value.astype(bf16)
        if quads[g]:
            for k in range(ring - 1, 0, -1):
                quad_copy(g, k).start()
        else:
            second_copy(g, 0).start()

    def gain(mask):
        return (1 - 2 * parity(me & (me ^ mask) & (n - PLANE), bits)).astype(f32) * scale

    gains = [gain(PLANE * k) for k in range(ring)]

    def turn_quad(g):
        some = second_in.at[:, :, down_rows(g)]
        remote(some, some, at_second + g, second_sem.at[g, 0], 0, PLANE).wait_recv()
        for b in range(2 * groups[g][0], 2 * groups[g][1]):
            columns = pl.ds(b * COLS, COLS)
            value = middle[:, columns] * gains[0]
            for k in range(1, ring):
                value = value + second_in[k - 1, :, columns].astype(f32) * gains[k]
            rotated[:, columns] = value.astype(bf16)

    def turn(g, level):
        lo, hi = groups[g]
        second_copy(g, level).wait_recv()
        for b in range(2 * lo, 2 * hi):
            columns = pl.ds(b * COLS, COLS)
            value = middle[:, columns] * line_flips[level]
            value = value + second_in[level, :, columns].astype(f32)
            if level == levels - 1:
                rotated[:, columns] = (value * scale).astype(bf16)
            else:
                middle[:, columns] = value
                second_out[level + 1, :, columns] = value.astype(bf16)
        if level < levels - 1:
            second_copy(g, level + 1).start()

    for b in range(blocks):
        block(b, *project(b))
        if b >= LAG:
            join(b - LAG)
    for b in range(max(blocks - LAG, 0), blocks):
        join(b)

    steps = [(0.6 * hi + 3.0 * stage, stage, g) for stage in range(levels) for g, (_, hi) in enumerate(groups)]
    for _, stage, g in sorted(steps):
        if stage:
            if not quads[g]:
                turn(g, stage - 1)
        else:
            meet(g)

    def rotate(g):
        if quads[g]:
            turn_quad(g)
        else:
            turn(g, levels - 1)
        some = downs.at[down_rows(g)]
        pltpu.make_async_copy(some, some, down_sem.at[g]).wait()

    def product(g, columns):
        return jnp.dot(rotated[:, down_rows(g)], downs[down_rows(g), columns], preferred_element_type=f32)

    final = len(groups) - 1
    for place, g in enumerate(sorted(range(final), key=lambda g: (not quads[g], g))):
        rotate(g)
        for c in range(outs // WIDE):
            columns = pl.ds(c * WIDE, WIDE)
            term = product(g, columns)
            if place:
                term = acc[:, columns] + term
            acc[:, columns] = term

    size = outs // CHUNKS
    half = total // 2
    pieces = n // 2
    place = me >> 1
    kept = pl.ds(pl.multiple_of((me & 1) * half, half), half)
    given = pl.ds(pl.multiple_of((1 - (me & 1)) * half, half), half)

    def half_copy(c):
        columns = pl.ds(c * size, size)
        return remote(half_out.at[:, columns], half_in.at[:, columns], at_half, half_sem.at[c], 0, 1)

    rotate(final)
    for c in range(CHUNKS):
        columns = pl.ds(c * size, size)
        for d in range(size // WIDE):
            narrow = pl.ds(c * size + d * WIDE, WIDE)
            acc[:, narrow] = acc[:, narrow] + product(final, narrow)
        half_out[:, columns] = acc[given, columns].astype(bf16)
        half_copy(c).start()
    for c in range(CHUNKS):
        columns = pl.ds(c * size, size)
        half_copy(c).wait_recv()
        term = acc[kept, columns] + half_in[:, columns].astype(f32)
        piece_out[:, :, columns] = term.astype(bf16).reshape(pieces, own, size)
        for k in range(pieces - 1, 0, -1):
            remote(
                piece_out.at[place ^ k, :, columns],
                piece_in.at[k, :, columns],
                at_piece,
                piece_sem.at[c],
                0,
                2 * k,
            ).start()
    others = pl.ds(1, pieces - 1)
    for c in range(CHUNKS):
        columns = pl.ds(c * size, size)
        some = piece_in.at[others, :, columns]
        remote(some, some, at_piece, piece_sem.at[c], 0, 2).wait_recv()
        term = piece_out[place, :, columns].astype(f32)
        for k in range(1, pieces):
            term = term + piece_in[k, :, columns].astype(f32)
        result[:, columns] = term.astype(bf16)
        pltpu.make_async_copy(result.at[:, columns], out.at[:, columns], own_sem.at[1]).start()
    pltpu.make_async_copy(result, out, own_sem.at[1]).wait()

    for which, some in [
        (at_gather, gathered.at[pl.ds(0, len(sends))]),
        (at_core, core_out),
        (at_first, first_in),
        (at_half, half_out),
        (at_piece, piece_in.at[others]),
    ]:
        remote(some, some, which, core_sem.at[0], 0, 1).wait_send()
    for g in every:
        some = (second_in if quads[g] else second_out).at[:, :, down_rows(g)]
        remote(some, some, at_second + g, core_sem.at[0], 0, 1).wait_send()


def fused(n, tokens, gate_weight, up_weight, down_weight):
    own, depth = tokens.shape
    total = n * own
    part = gate_weight.shape[1] // 2
    blocks = part // COLS
    outs = down_weight.shape[1]
    ring = n // PLANE
    levels = ring.bit_length() - 1
    pieces = n // 2
    groups = pl.cdiv(blocks, GROUP)
    bf16, f32 = jnp.bfloat16, jnp.float32
    anywhere = pl.BlockSpec(memory_space=pl.ANY)
    dma = pltpu.SemaphoreType.DMA
    return pl.pallas_call(
        functools.partial(kernel, n),
        out_shape=jax.ShapeDtypeStruct((own, outs), bf16),
        in_specs=[anywhere] * 4,
        out_specs=anywhere,
        scratch_shapes=[
            pltpu.VMEM((2 * n, own, depth), bf16),
            pltpu.VMEM((2 * total, depth), bf16),
            pltpu.VMEM((total, outs), f32),
            pltpu.VMEM((blocks, depth, 2 * COLS), bf16),
            pltpu.VMEM((2 * part, outs), bf16),
            pltpu.VMEM((COLS, COLS), bf16),
            pltpu.VMEM((2, total, part), f32),
            pltpu.VMEM((2, total, part), bf16),
            pltpu.VMEM((2, total, part), bf16),
            pltpu.VMEM((2, total, part), bf16),
            pltpu.VMEM((3, total, part), bf16),
            pltpu.VMEM((total, 2 * part), f32),
            pltpu.VMEM((levels, total, 2 * part), bf16),
            pltpu.VMEM((ring - 1, total, 2 * part), bf16),
            pltpu.VMEM((total, 2 * part), bf16),
            pltpu.VMEM((own, outs), bf16),
            pltpu.VMEM((total // 2, outs), bf16),
            pltpu.VMEM((total // 2, outs), bf16),
            pltpu.VMEM((pieces, own, outs), bf16),
            pltpu.VMEM((pieces, own, outs), bf16),
            dma((groups,)),
            dma((groups,)),
            dma((2 * ring + 2,)),
            dma((blocks,)),
            dma((groups,)),
            dma((groups, levels)),
            dma((CHUNKS,)),
            dma((CHUNKS,)),
            dma((5 + groups,)),
            dma((2,)),
            pltpu.SemaphoreType.REGULAR,
        ],
        compiler_params=pltpu.CompilerParams(
            collective_id=0, has_side_effects=True, vmem_limit_bytes=67_000_000
        ),
    )(tokens, gate_weight, up_weight, down_weight)


def per_device(tokens, gate_weight, up_weight, down_weight):
    n, parts = lax.axis_size("tensor"), lax.axis_size("groups")
    own, depth = tokens.shape
    width, outs = gate_weight.shape[1], down_weight.shape[1]
    total = n * own
    held = 2 * (width * (depth + outs) + 4 * total * (depth + outs) + 20 * total * width)
    fits = (
        parts == 2
        and n in (8, 16)
        and width % (2 * COLS) == 0
        and width // (2 * COLS) > GROUP
        and total % 32 == 0
        and total <= 64
        and depth % (1024 * SPLIT) == 0
        and outs % (2048 * CHUNKS) == 0
        and held <= 68_000_000
    )
    if fits:
        return fused(n, tokens, gate_weight, up_weight, down_weight)
    return plain(tokens, gate_weight, up_weight, down_weight)


def solution(mesh):
    return jax.shard_map(
        per_device,
        mesh=mesh,
        in_specs=(
            P(("groups", "tensor"), None),
            P(None, "tensor"),
            P(None, "tensor"),
            P("tensor", None),
        ),
        out_specs=P(("groups", "tensor"), None),
        check_vma=False,
    )
```

```python
import functools

import jax
import jax.numpy as jnp
import numpy as np
from jax import lax
from jax.experimental import pallas as pl
from jax.experimental.pallas import tpu as pltpu
from jax.sharding import PartitionSpec as P

BLOCK = 32
COLS = 128
SPLIT = 4
CHUNKS = 4
GROUP = 2
LAG = 2
QUADS = (0, 2, 3)
WIDE = 128
PLANE = 4
MESH = pl.DeviceIdType.MESH


def swapped(value, axis, stride):
    mask = 2**stride
    pairs = [(source, source ^ mask) for source in range(lax.axis_size(axis))]
    return lax.ppermute(value, axis, pairs)


def walsh(order):
    index = np.arange(order)
    common = index[:, None] & index[None, :]
    parity = common * 0
    for shift in range(max(order.bit_length(), 1)):
        parity = parity ^ common >> shift & 1
    return (1 - 2 * parity).astype(np.float32)


def plain(tokens, gate_weight, up_weight, down_weight):
    devices = lax.axis_size("tensor")
    width = gate_weight.shape[1]
    scale = 1.0 / np.sqrt(devices * BLOCK)
    inner = jnp.asarray(walsh(BLOCK), jnp.float32)
    piece = lax.all_gather(tokens, "tensor", axis=0, tiled=True)
    gate = jnp.dot(piece, gate_weight, preferred_element_type=jnp.float32)
    up = jnp.dot(piece, up_weight, preferred_element_type=jnp.float32)
    hidden = jax.nn.silu(gate) * up
    total = hidden.shape[0]
    local = jnp.einsum(
        "tbr,rs->tbs",
        hidden.reshape(total, width // BLOCK, BLOCK),
        inner,
        precision=lax.Precision.HIGHEST,
    ).reshape(total, width)
    index = lax.axis_index("tensor")
    for level in range(devices.bit_length() - 1):
        partner = swapped(local.astype(jnp.bfloat16), "tensor", level).astype(local.dtype)
        upper = index // (1 << level) % 2
        local = jnp.where(upper == 1, partner - local, local + partner)
    rotated = (local * scale).astype(jnp.bfloat16)
    terms = jnp.dot(rotated, down_weight, preferred_element_type=jnp.float32)
    mixed = lax.psum_scatter(terms, "tensor", scatter_dimension=0, tiled=True)
    return mixed.astype(jnp.bfloat16)


def parity(value, bits):
    total = value & 1
    for shift in range(1, bits):
        total = total ^ ((value >> shift) & 1)
    return total


def kernel(
    n,
    tokens,
    gate,
    up,
    down,
    out,
    gathered,
    lhs,
    acc,
    weights,
    downs,
    signs,
    hidden,
    core_out,
    core_in,
    first_out,
    first_in,
    middle,
    second_out,
    second_in,
    rotated,
    result,
    half_out,
    half_in,
    piece_out,
    piece_in,
    weight_sem,
    down_sem,
    gather_sem,
    core_sem,
    first_sem,
    second_sem,
    half_sem,
    piece_sem,
    send_sem,
    own_sem,
    known,
):
    f32, bf16 = jnp.float32, jnp.bfloat16
    me = lax.axis_index("tensor")
    mine = lax.axis_index("groups")
    own, depth = tokens.shape
    total = n * own
    part = gate.shape[1] // 2
    blocks = part // COLS
    outs = down.shape[1]
    bits = n.bit_length() - 1
    ring = n // PLANE
    levels = ring.bit_length() - 1
    scale = float(1.0 / np.sqrt(n * BLOCK))
    deep = depth // SPLIT
    groups = [(lo, min(lo + GROUP, blocks)) for lo in range(0, blocks, GROUP)]
    every = range(len(groups))
    at_gather, at_core, at_first, at_half, at_piece, at_second = range(6)
    quads = [g in QUADS or levels == 1 for g in every]

    def device(j, mask):
        return {"groups": mine ^ j, "tensor": me ^ mask}

    def slot(j, mask):
        q = me ^ mask
        return (mine ^ j) * n + (q & 1) * (n // 2) + (q >> 1)

    def remote(source, target, sent, received, j, mask):
        return pltpu.make_async_remote_copy(
            src_ref=source,
            dst_ref=target,
            send_sem=send_sem.at[sent],
            recv_sem=received,
            device_id=device(j, mask),
            device_id_type=MESH,
        )

    plane = [(j, m) for j in range(2) for m in range(PLANE) if j or m]
    line = [(0, PLANE * k) for k in range(1, ring)]

    barrier = pltpu.get_barrier_semaphore()
    greeted = plane + line[:2]
    for j, mask in greeted:
        pl.semaphore_signal(barrier, inc=1, device_id=device(j, mask), device_id_type=MESH)
    loaded = pltpu.make_async_copy(tokens, gathered.at[slot(0, 0)], own_sem.at[0])
    loaded.start()
    loaded.wait()

    for g, (lo, hi) in enumerate(groups):
        for b in range(lo, hi):
            start = pl.multiple_of(mine * part + b * COLS, COLS)
            for which, source in enumerate((gate, up)):
                pltpu.make_async_copy(
                    source.at[:, pl.ds(start, COLS)],
                    weights.at[b, :, pl.ds(which * COLS, COLS)],
                    weight_sem.at[g],
                ).start()

    def down_rows(g):
        lo, hi = groups[g]
        return pl.ds(2 * lo * COLS, 2 * (hi - lo) * COLS)

    def start_downs():
        for g, (lo, hi) in enumerate(groups):
            for b in range(lo, hi):
                for j in range(2):
                    start = pl.multiple_of((mine ^ j) * part + b * COLS, COLS)
                    pltpu.make_async_copy(
                        down.at[pl.ds(start, COLS)],
                        downs.at[pl.ds((2 * b + j) * COLS, COLS)],
                        down_sem.at[g],
                    ).start()

    pl.semaphore_wait(barrier, len(greeted))
    for j, mask in line[2:]:
        pl.semaphore_signal(known, inc=1, device_id=device(0, PLANE), device_id_type=MESH)

    near = [(1, 0), (0, 2), (1, 2)]
    across = near[:2]
    diagonal = near[2]
    ours = ring
    aside = 2 * ring
    last_sem = 2 * ring + 1
    kinds = {}
    for k in range(ring):
        for j, m in [(0, 0)] + near:
            if (j, m) == (0, 0):
                kind = k
            elif (j, m) != diagonal:
                kind = ours + k
            else:
                kind = aside if k else 0
            kinds[j, PLANE * k + m] = kind
            kinds[j, PLANE * k + m ^ 1] = last_sem
    sends = []

    def send(origin, j, mask):
        place = slot(*origin)
        kind = kinds[origin[0] ^ j, origin[1] ^ mask]
        remote(gathered.at[place], gathered.at[place], at_gather, gather_sem.at[kind], j, mask).start()
        sends.append(origin)

    def arrived(kind, count):
        some = gathered.at[pl.ds(0, count)]
        remote(some, some, at_gather, gather_sem.at[kind], 0, 1).wait_recv()

    for j, mask in [diagonal] + line[:2][::-1] + across + [(0, 1)]:
        send((0, 0), j, mask)
    for j, mask in line[2:]:
        pl.semaphore_wait(known, 1)
        send((0, 0), j, mask)

    one = lax.broadcasted_iota(jnp.int32, (COLS, COLS), 0)
    two = lax.broadcasted_iota(jnp.int32, (COLS, COLS), 1)
    sign = (1 - 2 * parity(one & two & (BLOCK - 1), BLOCK.bit_length() - 1)).astype(f32)
    signs[...] = jnp.where((one // BLOCK) == (two // BLOCK), sign, 0.0).astype(bf16)

    def spread(k):
        arrived(k, 1)
        for j, mask in across:
            send((0, PLANE * k), j, mask)
        if k == ring - 1:
            for j, mask in across:
                send((0, PLANE * k), j, mask ^ 1)
        send((0, PLANE * k), 0, 1)

    def from_across(k):
        arrived(ours + k, 2)
        if k == 0 or k < ring - 1:
            for j, mask in across:
                send((j, PLANE * k + mask), 0, 1)

    spread(1)
    arrived(0, 1)
    for j, mask in line[::-1] + [(0, 1)]:
        send(diagonal, j, mask)
    from_across(0)
    for k in range(2, ring):
        spread(k)
    start_downs()
    for k in range(1, ring):
        from_across(k)
    arrived(aside, ring - 1)
    for k in range(1, ring):
        send((diagonal[0], PLANE * k + diagonal[1]), 0, 1)
    arrived(last_sem, n)

    for g, (lo, hi) in enumerate(groups):
        some = weights.at[lo:hi]
        pltpu.make_async_copy(some, some, weight_sem.at[g]).wait()

    @pl.loop(0, depth // 1024)
    def _(c):
        columns = pl.ds(pl.multiple_of(c * 1024, 1024), 1024)
        lhs[:, columns] = gathered[:, :, columns].reshape(2 * total, 1024)

    def core_copy(b):
        columns = pl.ds(b * COLS, COLS)
        return remote(
            core_out.at[:, :, columns], core_in.at[:, :, columns], at_core, core_sem.at[b], 0, 1
        )

    def first_columns(g):
        lo, hi = groups[g]
        return pl.ds(lo * COLS, (hi - lo) * COLS)

    def second_copy(g, level):
        columns = down_rows(g)
        return remote(
            second_out.at[level, :, columns],
            second_in.at[level, :, columns],
            at_second + g,
            second_sem.at[g, level],
            0,
            PLANE << level,
        )

    def quad_copy(g, k):
        columns = down_rows(g)
        return remote(
            second_out.at[0, :, columns],
            second_in.at[k - 1, :, columns],
            at_second + g,
            second_sem.at[g, 0],
            0,
            PLANE * k,
        )

    def flip(mask):
        return (1 - 2 * parity(me & mask, bits)).astype(f32)

    core_flip, row_flip = flip(1), flip(2)
    line_flips = [flip(PLANE << level) for level in range(levels)]

    def project(b):
        left = jnp.zeros((2 * total, COLS), f32)
        right = jnp.zeros((2 * total, COLS), f32)
        for piece in range(SPLIT):
            rows_of = pl.ds(piece * deep, deep)
            left += jnp.dot(lhs[:, rows_of], weights[b, rows_of, :COLS], preferred_element_type=f32)
            right += jnp.dot(lhs[:, rows_of], weights[b, rows_of, COLS:], preferred_element_type=f32)
        return left, right

    def block(b, left, right):
        value = left / (1.0 + jnp.exp(-left)) * right
        high = value.astype(bf16)
        low = (value - high.astype(f32)).astype(bf16)
        value = jnp.dot(high, signs[...], preferred_element_type=f32) + jnp.dot(
            low, signs[...], preferred_element_type=f32
        )
        columns = pl.ds(b * COLS, COLS)
        for j in range(2):
            hidden[j, :, columns] = value[j * total : (j + 1) * total]
            core_out[j, :, columns] = value[j * total : (j + 1) * total].astype(bf16)
        core_copy(b).start()

    def join(b):
        core_copy(b).wait_recv()
        columns = pl.ds(b * COLS, COLS)
        for j in range(2):
            value = hidden[j, :, columns] * core_flip + core_in[j, :, columns].astype(f32)
            hidden[j, :, columns] = value
            first_out[j, :, columns] = value.astype(bf16)
        for g, (lo, hi) in enumerate(groups):
            if b == hi - 1:
                for place in (2, 0, 1):
                    j, m = near[place]
                    remote(
                        first_out.at[mine ^ j, :, first_columns(g)],
                        first_in.at[place, :, first_columns(g)],
                        at_first,
                        first_sem.at[g],
                        j,
                        m,
                    ).start()

    def meet(g):
        some = first_in.at[:, :, first_columns(g)]
        remote(some, some, at_first, first_sem.at[g], 0, 1).wait_recv()
        for b in range(*groups[g]):
            columns = pl.ds(b * COLS, COLS)
            pair = [
                hidden[mine, :, columns] * row_flip + first_in[1, :, columns].astype(f32),
                first_in[0, :, columns].astype(f32) * row_flip + first_in[2, :, columns].astype(f32),
            ]
            for j, value in enumerate(pair):
                target = pl.ds((2 * b + j) * COLS, COLS)
                middle[:, target] = value
                second_out[0, :, target] = value.astype(bf16)
        if quads[g]:
            for k in range(ring - 1, 0, -1):
                quad_copy(g, k).start()
        else:
            second_copy(g, 0).start()

    def gain(mask):
        return (1 - 2 * parity(me & (me ^ mask) & (n - PLANE), bits)).astype(f32) * scale

    gains = [gain(PLANE * k) for k in range(ring)]

    def turn_quad(g):
        some = second_in.at[:, :, down_rows(g)]
        remote(some, some, at_second + g, second_sem.at[g, 0], 0, PLANE).wait_recv()
        for b in range(2 * groups[g][0], 2 * groups[g][1]):
            columns = pl.ds(b * COLS, COLS)
            value = middle[:, columns] * gains[0]
            for k in range(1, ring):
                value = value + second_in[k - 1, :, columns].astype(f32) * gains[k]
            rotated[:, columns] = value.astype(bf16)

    def turn(g, level):
        lo, hi = groups[g]
        second_copy(g, level).wait_recv()
        for b in range(2 * lo, 2 * hi):
            columns = pl.ds(b * COLS, COLS)
            value = middle[:, columns] * line_flips[level]
            value = value + second_in[level, :, columns].astype(f32)
            if level == levels - 1:
                rotated[:, columns] = (value * scale).astype(bf16)
            else:
                middle[:, columns] = value
                second_out[level + 1, :, columns] = value.astype(bf16)
        if level < levels - 1:
            second_copy(g, level + 1).start()

    for b in range(blocks):
        block(b, *project(b))
        if b >= LAG:
            join(b - LAG)
    for b in range(max(blocks - LAG, 0), blocks):
        join(b)

    steps = [(0.6 * hi + 3.0 * stage, stage, g) for stage in range(levels) for g, (_, hi) in enumerate(groups)]
    for _, stage, g in sorted(steps):
        if stage:
            if not quads[g]:
                turn(g, stage - 1)
        else:
            meet(g)

    def rotate(g):
        if quads[g]:
            turn_quad(g)
        else:
            turn(g, levels - 1)
        some = downs.at[down_rows(g)]
        pltpu.make_async_copy(some, some, down_sem.at[g]).wait()

    def product(g, columns):
        return jnp.dot(rotated[:, down_rows(g)], downs[down_rows(g), columns], preferred_element_type=f32)

    final = len(groups) - 1
    for place, g in enumerate(sorted(range(final), key=lambda g: (not quads[g], g))):
        rotate(g)
        for c in range(outs // WIDE):
            columns = pl.ds(c * WIDE, WIDE)
            term = product(g, columns)
            if place:
                term = acc[:, columns] + term
            acc[:, columns] = term

    size = outs // CHUNKS
    half = total // 2
    pieces = n // 2
    place = me >> 1
    kept = pl.ds(pl.multiple_of((me & 1) * half, half), half)
    given = pl.ds(pl.multiple_of((1 - (me & 1)) * half, half), half)

    def half_copy(c):
        columns = pl.ds(c * size, size)
        return remote(half_out.at[:, columns], half_in.at[:, columns], at_half, half_sem.at[c], 0, 1)

    rotate(final)
    for c in range(CHUNKS):
        columns = pl.ds(c * size, size)
        for d in range(size // WIDE):
            narrow = pl.ds(c * size + d * WIDE, WIDE)
            acc[:, narrow] = acc[:, narrow] + product(final, narrow)
        half_out[:, columns] = acc[given, columns].astype(bf16)
        half_copy(c).start()
    for c in range(CHUNKS):
        columns = pl.ds(c * size, size)
        half_copy(c).wait_recv()
        term = acc[kept, columns] + half_in[:, columns].astype(f32)
        piece_out[:, :, columns] = term.astype(bf16).reshape(pieces, own, size)
        for k in range(pieces - 1, 0, -1):
            remote(
                piece_out.at[place ^ k, :, columns],
                piece_in.at[k, :, columns],
                at_piece,
                piece_sem.at[c],
                0,
                2 * k,
            ).start()
    others = pl.ds(1, pieces - 1)
    for c in range(CHUNKS):
        columns = pl.ds(c * size, size)
        some = piece_in.at[others, :, columns]
        remote(some, some, at_piece, piece_sem.at[c], 0, 2).wait_recv()
        term = piece_out[place, :, columns].astype(f32)
        for k in range(1, pieces):
            term = term + piece_in[k, :, columns].astype(f32)
        result[:, columns] = term.astype(bf16)
        pltpu.make_async_copy(result.at[:, columns], out.at[:, columns], own_sem.at[1]).start()
    pltpu.make_async_copy(result, out, own_sem.at[1]).wait()

    for which, some in [
        (at_gather, gathered.at[pl.ds(0, len(sends))]),
        (at_core, core_out),
        (at_first, first_in),
        (at_half, half_out),
        (at_piece, piece_in.at[others]),
    ]:
        remote(some, some, which, core_sem.at[0], 0, 1).wait_send()
    for g in every:
        some = (second_in if quads[g] else second_out).at[:, :, down_rows(g)]
        remote(some, some, at_second + g, core_sem.at[0], 0, 1).wait_send()


def fused(n, tokens, gate_weight, up_weight, down_weight):
    own, depth = tokens.shape
    total = n * own
    part = gate_weight.shape[1] // 2
    blocks = part // COLS
    outs = down_weight.shape[1]
    ring = n // PLANE
    levels = ring.bit_length() - 1
    pieces = n // 2
    groups = pl.cdiv(blocks, GROUP)
    bf16, f32 = jnp.bfloat16, jnp.float32
    anywhere = pl.BlockSpec(memory_space=pl.ANY)
    dma = pltpu.SemaphoreType.DMA
    return pl.pallas_call(
        functools.partial(kernel, n),
        out_shape=jax.ShapeDtypeStruct((own, outs), bf16),
        in_specs=[anywhere] * 4,
        out_specs=anywhere,
        scratch_shapes=[
            pltpu.VMEM((2 * n, own, depth), bf16),
            pltpu.VMEM((2 * total, depth), bf16),
            pltpu.VMEM((total, outs), f32),
            pltpu.VMEM((blocks, depth, 2 * COLS), bf16),
            pltpu.VMEM((2 * part, outs), bf16),
            pltpu.VMEM((COLS, COLS), bf16),
            pltpu.VMEM((2, total, part), f32),
            pltpu.VMEM((2, total, part), bf16),
            pltpu.VMEM((2, total, part), bf16),
            pltpu.VMEM((2, total, part), bf16),
            pltpu.VMEM((3, total, part), bf16),
            pltpu.VMEM((total, 2 * part), f32),
            pltpu.VMEM((levels, total, 2 * part), bf16),
            pltpu.VMEM((ring - 1, total, 2 * part), bf16),
            pltpu.VMEM((total, 2 * part), bf16),
            pltpu.VMEM((own, outs), bf16),
            pltpu.VMEM((total // 2, outs), bf16),
            pltpu.VMEM((total // 2, outs), bf16),
            pltpu.VMEM((pieces, own, outs), bf16),
            pltpu.VMEM((pieces, own, outs), bf16),
            dma((groups,)),
            dma((groups,)),
            dma((2 * ring + 2,)),
            dma((blocks,)),
            dma((groups,)),
            dma((groups, levels)),
            dma((CHUNKS,)),
            dma((CHUNKS,)),
            dma((5 + groups,)),
            dma((2,)),
            pltpu.SemaphoreType.REGULAR,
        ],
        compiler_params=pltpu.CompilerParams(
            collective_id=0, has_side_effects=True, vmem_limit_bytes=67_000_000
        ),
    )(tokens, gate_weight, up_weight, down_weight)


def per_device(tokens, gate_weight, up_weight, down_weight):
    n, parts = lax.axis_size("tensor"), lax.axis_size("groups")
    own, depth = tokens.shape
    width, outs = gate_weight.shape[1], down_weight.shape[1]
    total = n * own
    held = 2 * (width * (depth + outs) + 4 * total * (depth + outs) + 20 * total * width)
    fits = (
        parts == 2
        and n in (8, 16)
        and width % (2 * COLS) == 0
        and width // (2 * COLS) > GROUP
        and total % 32 == 0
        and total <= 64
        and depth % (1024 * SPLIT) == 0
        and outs % (2048 * CHUNKS) == 0
        and held <= 68_000_000
    )
    if fits:
        return fused(n, tokens, gate_weight, up_weight, down_weight)
    return plain(tokens, gate_weight, up_weight, down_weight)


def solution(mesh):
    return jax.shard_map(
        per_device,
        mesh=mesh,
        in_specs=(
            P(("groups", "tensor"), None),
            P(None, "tensor"),
            P(None, "tensor"),
            P("tensor", None),
        ),
        out_specs=P(("groups", "tensor"), None),
        check_vma=False,
    )
```
